32 devices in a mesh: clip: 2 (over y), tile: 4 (over z), frame: 2 (over x), chan: 2 (over core).
Axes of the slice: x: 2, y: 2, z: 4, core: 2. Of those that a mesh axis runs over, the one named last changes fastest.
Arguments:
- features: bfloat16 [4, 8, 256, 256], P(('clip', 'frame'), 'tile', None, 'chan'), parts along dimension 0, may hold values from -6 to 6
- neighbours: int32 [16, 9], P(('clip', 'tile')), parts along dimension 0, may hold values from 0 to 7, as said below
- pairing: int32 [4, 2], P(('clip', 'frame')), parts along dimension 0, may hold values 0 or 1
- valid_tiles: int32 [16, 256], P(('clip', 'tile')), parts along dimension 0, may hold values 0 or 1
- cotangent: bfloat16 [4, 8, 256, 3060], P(('clip', 'frame'), 'tile', 'chan'), parts along dimension 0, may hold values from -6 to 6
Outputs:
- volume: bfloat16 [4, 8, 256, 3060], P(('clip', 'frame'), 'tile', 'chan'), parts along dimension 0
- feature_grad: float32 [4, 8, 256, 256], P(('clip', 'frame'), 'tile', None, 'chan'), parts along dimension 0
The draws below stay inside these ranges and needn't reach their ends.
There are 2 independent parts, one for each index of `clip`. The reference program is written for one: setup_inputs(seed, part) draws one part's arguments, and reference() takes and returns one part's arrays. A program takes and returns all parts, laid end to end along the dimension named above; each array names one. Nothing has to cross between parts.
Inputs may be any that keep to these rules, and one draw needn't show every extreme that they name: `neighbours`: every entry of row a lies within 2 tiles of a, and in every row one entry lies exactly 2 tiles from a.
All inputs are finite; a program needn't handle non-finite values. No bound on the sum of `pairing` or of `valid_tiles` on one device may be relied on, other than what follows from the above.
Results may differ from the reference program's by a relative error of at most 0.008.
Values may be sent and summed in bfloat16 or wider, within the bound.
A program may use at most 64 MiB of HBM per device.

```python
import math
import jax
import jax.numpy as jnp
from jax import lax

CHANNELS = 256
SIDE = 16
PIXELS = 256
LEVELS = 340
NEIGHBOURS = 9
TILE_DEV = 2
TILES = 8
FRAMES = 2


def draw_neighbours(key, part):
    tile_ids = jnp.arange(TILES, dtype=jnp.int32)[:, None]
    offsets = jax.random.randint(key, (TILES, NEIGHBOURS), -TILE_DEV, TILE_DEV + 1).astype(jnp.int32)
    farthest = jnp.where(tile_ids + TILE_DEV < TILES, TILE_DEV, -TILE_DEV).astype(jnp.int32)
    offsets = offsets.at[:, 0].set(farthest[:, 0])
    return jnp.clip(tile_ids + offsets, 0, TILES - 1).astype(jnp.int32)


def with_ends(array, rng, least, high):
    longest = array.shape.index(max(array.shape))
    spots = []
    for shift in (0, 1):
        where = [jax.random.randint(jax.random.fold_in(rng, axis), (), 0, length) for axis, length in enumerate(array.shape)]
        where[longest] = (where[longest] + shift) % array.shape[longest]
        spots.append(tuple(where))
    return array.at[spots[0]].set(least).at[spots[1]].set(high)


def block_levels(own_key, dims, cuts, least, top_value):
    gain, own = 1.0, jax.random.fold_in(own_key, 6)
    for axis_at, blocks in cuts:
        heights = jnp.exp(jax.random.uniform(jax.random.fold_in(own, axis_at), (blocks,), jnp.float32, least / len(cuts), top_value / len(cuts)))
        gain = gain * jnp.repeat(heights, dims[axis_at] // blocks).reshape([-1 if axis == axis_at else 1 for axis in range(len(dims))])
    return gain


def bell_draw(own_key, shape, scale, most, split=(), kind=jnp.bfloat16):
    gain = block_levels(own_key, shape, split, -0.22, 0.18) if split else 1.0
    entries = jax.random.normal(own_key, shape, jnp.float32) * scale * gain
    return jnp.minimum(jnp.maximum(entries, -most), most).astype(kind)


def setup_inputs(seed: int = 0, part: int = 0) -> dict:
    splits = jax.random.split(jax.random.key(seed), 6)
    part_splits = jax.random.split(jax.random.fold_in(splits[5], part), 6)
    return {
        "features": bell_draw(part_splits[0], (FRAMES, TILES, PIXELS, CHANNELS), 1.0, 6.0, ((0, 2), (1, 4), (3, 2))),
        "neighbours": draw_neighbours(jax.random.fold_in(jax.random.fold_in(splits[5], part), 71), part),
        "pairing": with_ends((jax.random.randint(part_splits[2], (FRAMES, 2), 0, 4) < 3).astype(jnp.int32), jax.random.fold_in(part_splits[2], 1), 0, 1),
        "valid_tiles": with_ends((jax.random.randint(part_splits[3], (TILES, PIXELS), 0, 4) < 3).astype(jnp.int32), jax.random.fold_in(part_splits[3], 1), 0, 1),
        "cotangent": bell_draw(part_splits[4], (FRAMES, TILES, PIXELS, NEIGHBOURS * LEVELS), 1.0, 6.0, ((0, 2), (1, 4), (2, 2))),
    }


def pyramid_of(float_features):
    grid_view = float_features.reshape(FRAMES, TILES, SIDE, SIDE, CHANNELS)
    levels = []
    for extent in (1, 2, 4, 8):
        across = SIDE // extent
        pooled = grid_view.reshape(FRAMES, TILES, across, extent, across, extent, CHANNELS).mean(axis=(3, 5))
        levels.append(pooled.reshape(FRAMES, TILES, across * across, CHANNELS))
    pooled = jnp.concatenate(levels, 2)
    rounded = lax.optimization_barrier(pooled.astype(jnp.bfloat16)).astype(pooled.dtype)
    return pooled + lax.stop_gradient(rounded - pooled)

def correlate(float_features, neighbours, pairing, valid_tiles):
    pyramid = pyramid_of(float_features)
    blank_frame = jnp.zeros_like(pyramid[:1])
    before = jnp.concatenate([blank_frame, pyramid[:-1]], 0)
    following = jnp.concatenate([pyramid[1:], blank_frame], 0)
    summed = jnp.zeros((FRAMES, TILES, PIXELS, NEIGHBOURS, LEVELS), float_features.dtype)
    for partner_index, partner in enumerate((before, following)):
        chosen = partner[:, neighbours]
        scores = jnp.einsum('fapc,fakmc->fapkm', float_features, chosen, precision=lax.Precision.HIGHEST)
        gate = pairing[:, partner_index].astype(float_features.dtype)[:, None, None, None, None]
        summed = summed + gate * scores
    summed = summed * (valid_tiles.astype(float_features.dtype)[None, :, :, None, None] / math.sqrt(CHANNELS))
    return summed.reshape(FRAMES, TILES, PIXELS, NEIGHBOURS * LEVELS)

def reference(features, neighbours, pairing, valid_tiles, cotangent):
    float_features = features.astype(jnp.float32)

    def forward(values):
        return correlate(values, neighbours, pairing, valid_tiles)
    volume, pullback = jax.vjp(forward, float_features)
    feature_grad, = pullback(cotangent.astype(jnp.float32))
    return (volume.astype(jnp.bfloat16), feature_grad)
```

```python
import math

import jax
import jax.numpy as jnp
from jax import lax
from jax.sharding import PartitionSpec as P

CHANNELS = 256
SIDE = 16
PIXELS = 256
LEVELS = 340
NEIGHBOURS = 9
EXTENTS = (1, 2, 4, 8)


def shift(x, axis, step):
    count = lax.axis_size(axis)
    if step > 0:
        pairs = [(i, i + 1) for i in range(count - 1)]
    else:
        pairs = [(i + 1, i) for i in range(count - 1)]
    return lax.ppermute(x, axis, pairs)


def pool_weights_table():
    pixel_ids = jnp.arange(PIXELS, dtype=jnp.int32)
    row_of = pixel_ids // SIDE
    column = pixel_ids % SIDE
    pieces = []
    for extent in EXTENTS:
        across = SIDE // extent
        target = row_of // extent * across + column // extent
        member = jnp.arange(across * across, dtype=jnp.int32)[:, None] == target[None, :]
        pieces.append(member.astype(jnp.float32) / (extent * extent))
    return jnp.concatenate(pieces, 0)


def pool_back(cells):
    lead = cells.shape[0]
    chans = cells.shape[-1]
    total = None
    start = 0
    for extent in EXTENTS:
        across = SIDE // extent
        part = cells[:, start : start + across * across] * (1.0 / (extent * extent))
        start += across * across
        part = part.reshape(lead, across, 1, across, 1, chans)
        part = jnp.broadcast_to(part, (lead, across, extent, across, extent, chans))
        part = part.reshape(lead, PIXELS, chans)
        total = part if total is None else total + part
    return total


def local(features, neighbours, pairing, valid_tiles, cotangent):
    tile_count = features.shape[1]
    half_rows = cotangent.shape[2]
    pool_weights = pool_weights_table()
    present = lax.all_gather(features, "chan", axis=3, tiled=True)[0]
    before = shift(present, "frame", 1)
    after = shift(present, "frame", -1)
    partners = jnp.stack([before, after], 0)
    window = jnp.concatenate(
        [shift(partners, "tile", 1), partners, shift(partners, "tile", -1)], axis=1
    )
    pyramid = jnp.einsum(
        "mp,jwpc->jwmc",
        pool_weights.astype(jnp.bfloat16),
        window,
        preferred_element_type=jnp.float32,
    ).astype(jnp.bfloat16)
    gate01 = pairing[0].astype(jnp.bfloat16)
    pyramid = pyramid * gate01[:, None, None, None]
    core_index = lax.axis_index("chan")
    queries = lax.dynamic_slice_in_dim(present, core_index * half_rows, half_rows, 1)
    valid_local = lax.dynamic_slice_in_dim(valid_tiles, core_index * half_rows, half_rows, 1)
    scale = valid_local.astype(jnp.float32) * (1.0 / math.sqrt(CHANNELS))
    slot_ids = neighbours - (lax.axis_index("tile") * tile_count - tile_count)
    chosen = pyramid[:, slot_ids]
    queries2 = jnp.broadcast_to(queries[None], (2,) + queries.shape)
    scores = jnp.einsum(
        "jakmc,japc->kmap", chosen, queries2, preferred_element_type=jnp.float32
    )
    summed = scores * scale[None, None]
    volume = summed.reshape(NEIGHBOURS * LEVELS, tile_count, half_rows).astype(jnp.bfloat16)
    volume = jnp.transpose(volume, (1, 2, 0))[None]
    upstream = cotangent[0].reshape(tile_count, half_rows, NEIGHBOURS, LEVELS)
    upstream = upstream * valid_local.astype(jnp.bfloat16)[:, :, None, None]
    partial_query = jnp.einsum(
        "apkm,jakmc->japc", upstream, chosen, preferred_element_type=jnp.float32
    )
    query_grad = jnp.sum(partial_query, axis=0) * (1.0 / math.sqrt(CHANNELS))
    base_grad = jnp.einsum("apkm,apc->akmc", upstream, queries, preferred_element_type=jnp.float32)
    member = (
        slot_ids[:, :, None] == jnp.arange(3 * tile_count, dtype=jnp.int32)[None, None, :]
    ).astype(jnp.float32)
    cells = jnp.sum(member[:, :, :, None, None] * base_grad[:, :, None], axis=(0, 1))
    window_grad = pool_back(cells)
    sent_left = shift(window_grad[:tile_count].astype(jnp.bfloat16), "tile", -1)
    sent_right = shift(window_grad[2 * tile_count :].astype(jnp.bfloat16), "tile", 1)
    returned = (
        sent_left.astype(jnp.float32)
        + window_grad[tile_count : 2 * tile_count]
        + sent_right.astype(jnp.float32)
    )
    gates = pairing[0].astype(jnp.float32) * (1.0 / math.sqrt(CHANNELS))
    from_next = shift((returned * gates[0]).astype(jnp.bfloat16), "frame", -1)
    from_prev = shift((returned * gates[1]).astype(jnp.bfloat16), "frame", 1)
    key_grad = from_prev.astype(jnp.float32) + from_next.astype(jnp.float32)
    placed = lax.dynamic_update_slice_in_dim(
        jnp.zeros(key_grad.shape, jnp.float32), query_grad, core_index * half_rows, 1
    )
    feature_grad = lax.psum_scatter(key_grad + placed, "chan", scatter_dimension=2, tiled=True)
    return (volume, feature_grad[None])


def solution(mesh):
    return jax.shard_map(
        local,
        mesh=mesh,
        in_specs=(
            P(("clip", "frame"), "tile", None, "chan"),
            P(("clip", "tile"), None),
            P(("clip", "frame"), None),
            P(("clip", "tile"), None),
            P(("clip", "frame"), "tile", "chan", None),
        ),
        out_specs=(
            P(("clip", "frame"), "tile", "chan", None),
            P(("clip", "frame"), "tile", None, "chan"),
        ),
        check_vma=False,
    )
```

```python
import math

import jax
import jax.numpy as jnp
from jax import lax
from jax.sharding import PartitionSpec as P

CHANNELS = 256
SIDE = 16
PIXELS = 256
LEVELS = 340
NEIGHBOURS = 9
EXTENTS = (1, 2, 4, 8)


def shift(x, axis, step):
    count = lax.axis_size(axis)
    if step > 0:
        pairs = [(i, i + 1) for i in range(count - 1)]
    else:
        pairs = [(i + 1, i) for i in range(count - 1)]
    return lax.ppermute(x, axis, pairs)


def pool_weights_table():
    pixel_ids = jnp.arange(PIXELS, dtype=jnp.int32)
    row_of = pixel_ids // SIDE
    column = pixel_ids % SIDE
    pieces = []
    for extent in EXTENTS:
        across = SIDE // extent
        target = row_of // extent * across + column // extent
        member = jnp.arange(across * across, dtype=jnp.int32)[:, None] == target[None, :]
        pieces.append(member.astype(jnp.float32) / (extent * extent))
    return jnp.concatenate(pieces, 0)


def pool_back(cells):
    lead = cells.shape[0]
    chans = cells.shape[-1]
    total = None
    start = 0
    for extent in EXTENTS:
        across = SIDE // extent
        part = cells[:, start : start + across * across] * (1.0 / (extent * extent))
        start += across * across
        part = part.reshape(lead, across, 1, across, 1, chans)
        part = jnp.broadcast_to(part, (lead, across, extent, across, extent, chans))
        part = part.reshape(lead, PIXELS, chans)
        total = part if total is None else total + part
    return total


def local(features, neighbours, pairing, valid_tiles, cotangent):
    tile_count = features.shape[1]
    half_rows = cotangent.shape[2]
    pool_weights = pool_weights_table()
    present = lax.all_gather(features, "chan", axis=3, tiled=True)[0]
    before = shift(present, "frame", 1)
    after = shift(present, "frame", -1)
    partners = jnp.stack([before, after], 0)
    window = jnp.concatenate(
        [shift(partners, "tile", 1), partners, shift(partners, "tile", -1)], axis=1
    )
    pyramid = jnp.einsum(
        "mp,jwpc->jwmc",
        pool_weights.astype(jnp.bfloat16),
        window,
        preferred_element_type=jnp.float32,
    ).astype(jnp.bfloat16)
    gate01 = pairing[0].astype(jnp.bfloat16)
    pyramid = pyramid * gate01[:, None, None, None]
    core_index = lax.axis_index("chan")
    queries = lax.dynamic_slice_in_dim(present, core_index * half_rows, half_rows, 1)
    valid_local = lax.dynamic_slice_in_dim(valid_tiles, core_index * half_rows, half_rows, 1)
    scale = valid_local.astype(jnp.float32) * (1.0 / math.sqrt(CHANNELS))
    slot_ids = neighbours - (lax.axis_index("tile") * tile_count - tile_count)
    chosen = pyramid[:, slot_ids]
    queries2 = jnp.broadcast_to(queries[None], (2,) + queries.shape)
    scores = jnp.einsum(
        "jakmc,japc->kmap", chosen, queries2, preferred_element_type=jnp.float32
    )
    summed = scores * scale[None, None]
    volume = summed.reshape(NEIGHBOURS * LEVELS, tile_count, half_rows).astype(jnp.bfloat16)
    volume = jnp.transpose(volume, (1, 2, 0))[None]
    upstream = cotangent[0].reshape(tile_count, half_rows, NEIGHBOURS, LEVELS)
    upstream = upstream * valid_local.astype(jnp.bfloat16)[:, :, None, None]
    partial_query = jnp.einsum(
        "apkm,jakmc->japc", upstream, chosen, preferred_element_type=jnp.float32
    )
    query_grad = jnp.sum(partial_query, axis=0) * (1.0 / math.sqrt(CHANNELS))
    base_grad = jnp.einsum("apkm,apc->akmc", upstream, queries, preferred_element_type=jnp.float32)
    member = (
        slot_ids[:, :, None] == jnp.arange(3 * tile_count, dtype=jnp.int32)[None, None, :]
    ).astype(jnp.float32)
    cells = None
    for a in range(tile_count):
        for k in range(NEIGHBOURS):
            term = member[a, k][:, None, None] * base_grad[a, k][None]
            cells = term if cells is None else cells + term
    window_grad = pool_back(cells)
    sent_left = shift(window_grad[:tile_count].astype(jnp.bfloat16), "tile", -1)
    sent_right = shift(window_grad[2 * tile_count :].astype(jnp.bfloat16), "tile", 1)
    returned = (
        sent_left.astype(jnp.float32)
        + window_grad[tile_count : 2 * tile_count]
        + sent_right.astype(jnp.float32)
    )
    gates = pairing[0].astype(jnp.float32) * (1.0 / math.sqrt(CHANNELS))
    from_next = shift((returned * gates[0]).astype(jnp.bfloat16), "frame", -1)
    from_prev = shift((returned * gates[1]).astype(jnp.bfloat16), "frame", 1)
    key_grad = from_prev.astype(jnp.float32) + from_next.astype(jnp.float32)
    placed = lax.dynamic_update_slice_in_dim(
        jnp.zeros(key_grad.shape, jnp.float32), query_grad, core_index * half_rows, 1
    )
    feature_grad = lax.psum_scatter(key_grad + placed, "chan", scatter_dimension=2, tiled=True)
    return (volume, feature_grad[None])


def solution(mesh):
    return jax.shard_map(
        local,
        mesh=mesh,
        in_specs=(
            P(("clip", "frame"), "tile", None, "chan"),
            P(("clip", "tile"), None),
            P(("clip", "frame"), None),
            P(("clip", "tile"), None),
            P(("clip", "frame"), "tile", "chan", None),
        ),
        out_specs=(
            P(("clip", "frame"), "tile", "chan", None),
            P(("clip", "frame"), "tile", None, "chan"),
        ),
        check_vma=False,
    )
```

```python
import math

import jax
import jax.numpy as jnp
from jax import lax
from jax.sharding import PartitionSpec as P

CHANNELS = 256
SIDE = 16
PIXELS = 256
LEVELS = 340
NEIGHBOURS = 9
EXTENTS = (1, 2, 4, 8)


def shift(x, axis, step):
    count = lax.axis_size(axis)
    if step > 0:
        pairs = [(i, i + 1) for i in range(count - 1)]
    else:
        pairs = [(i + 1, i) for i in range(count - 1)]
    return lax.ppermute(x, axis, pairs)


def shift2(x, frame_step, tile_step):
    frames = lax.axis_size("frame")
    tiles = lax.axis_size("tile")
    pairs = []
    for f in range(frames):
        for t in range(tiles):
            f2, t2 = f + frame_step, t + tile_step
            if 0 <= f2 < frames and 0 <= t2 < tiles:
                pairs.append((t * frames + f, t2 * frames + f2))
    return lax.ppermute(x, ("tile", "frame"), pairs)


def pool_weights_table():
    pixel_ids = jnp.arange(PIXELS, dtype=jnp.int32)
    row_of = pixel_ids // SIDE
    column = pixel_ids % SIDE
    pieces = []
    for extent in EXTENTS:
        across = SIDE // extent
        target = row_of // extent * across + column // extent
        member = jnp.arange(across * across, dtype=jnp.int32)[:, None] == target[None, :]
        pieces.append(member.astype(jnp.float32) / (extent * extent))
    return jnp.concatenate(pieces, 0)


def pool_back(cells):
    lead = cells.shape[0]
    chans = cells.shape[-1]
    total = None
    start = 0
    for extent in EXTENTS:
        across = SIDE // extent
        part = cells[:, start : start + across * across] * (1.0 / (extent * extent))
        start += across * across
        part = part.reshape(lead, across, 1, across, 1, chans)
        part = jnp.broadcast_to(part, (lead, across, extent, across, extent, chans))
        part = part.reshape(lead, PIXELS, chans)
        total = part if total is None else total + part
    return total


def local(features, neighbours, pairing, valid_tiles, cotangent):
    tile_count = features.shape[1]
    half_rows = cotangent.shape[2]
    pool_weights = pool_weights_table()
    present = lax.all_gather(features, "chan", axis=3, tiled=True)[0]
    rows = []
    for frame_step in (1, -1):
        rows.append(
            jnp.concatenate([shift2(present, frame_step, t) for t in (1, 0, -1)], axis=0)
        )
    window = jnp.stack(rows, 0)
    pyramid = jnp.einsum(
        "mp,jwpc->jwmc",
        pool_weights.astype(jnp.bfloat16),
        window,
        preferred_element_type=jnp.float32,
    ).astype(jnp.bfloat16)
    gate01 = pairing[0].astype(jnp.bfloat16)
    pyramid = pyramid * gate01[:, None, None, None]
    core_index = lax.axis_index("chan")
    queries = lax.dynamic_slice_in_dim(present, core_index * half_rows, half_rows, 1)
    valid_local = lax.dynamic_slice_in_dim(valid_tiles, core_index * half_rows, half_rows, 1)
    scale = valid_local.astype(jnp.float32) * (1.0 / math.sqrt(CHANNELS))
    slot_ids = neighbours - (lax.axis_index("tile") * tile_count - tile_count)
    chosen = pyramid[:, slot_ids]
    queries2 = jnp.broadcast_to(queries[None], (2,) + queries.shape)
    scores = jnp.einsum(
        "jakmc,japc->kmap", chosen, queries2, preferred_element_type=jnp.float32
    )
    summed = scores * scale[None, None]
    volume = summed.reshape(NEIGHBOURS * LEVELS, tile_count, half_rows).astype(jnp.bfloat16)
    volume = jnp.transpose(volume, (1, 2, 0))[None]
    upstream = cotangent[0].reshape(tile_count, half_rows, NEIGHBOURS, LEVELS)
    upstream = upstream * valid_local.astype(jnp.bfloat16)[:, :, None, None]
    partial_query = jnp.einsum(
        "apkm,jakmc->japc", upstream, chosen, preferred_element_type=jnp.float32
    )
    query_grad = jnp.sum(partial_query, axis=0) * (1.0 / math.sqrt(CHANNELS))
    base_grad = jnp.einsum("apkm,apc->akmc", upstream, queries, preferred_element_type=jnp.float32)
    member = (
        slot_ids[:, :, None] == jnp.arange(3 * tile_count, dtype=jnp.int32)[None, None, :]
    ).astype(jnp.float32)
    cells = None
    for a in range(tile_count):
        for k in range(NEIGHBOURS):
            term = member[a, k][:, None, None] * base_grad[a, k][None]
            cells = term if cells is None else cells + term
    window_grad = pool_back(cells)
    gates = pairing[0].astype(jnp.float32) * (1.0 / math.sqrt(CHANNELS))
    key_grad = None
    for j, frame_step in ((0, -1), (1, 1)):
        for block, tile_step in ((0, -1), (1, 0), (2, 1)):
            piece = window_grad[block * tile_count : (block + 1) * tile_count] * gates[j]
            got = shift2(piece.astype(jnp.bfloat16), frame_step, tile_step).astype(jnp.float32)
            key_grad = got if key_grad is None else key_grad + got
    placed = lax.dynamic_update_slice_in_dim(
        jnp.zeros(key_grad.shape, jnp.float32), query_grad, core_index * half_rows, 1
    )
    feature_grad = lax.psum_scatter(key_grad + placed, "chan", scatter_dimension=2, tiled=True)
    return (volume, feature_grad[None])


def solution(mesh):
    return jax.shard_map(
        local,
        mesh=mesh,
        in_specs=(
            P(("clip", "frame"), "tile", None, "chan"),
            P(("clip", "tile"), None),
            P(("clip", "frame"), None),
            P(("clip", "tile"), None),
            P(("clip", "frame"), "tile", "chan", None),
        ),
        out_specs=(
            P(("clip", "frame"), "tile", "chan", None),
            P(("clip", "frame"), "tile", None, "chan"),
        ),
        check_vma=False,
    )
```

```python
import math

import jax
import jax.numpy as jnp
from jax import lax
from jax.sharding import PartitionSpec as P

CHANNELS = 256
SIDE = 16
PIXELS = 256
LEVELS = 340
NEIGHBOURS = 9
EXTENTS = (1, 2, 4, 8)


def shift(x, axis, step):
    count = lax.axis_size(axis)
    if step > 0:
        pairs = [(i, i + 1) for i in range(count - 1)]
    else:
        pairs = [(i + 1, i) for i in range(count - 1)]
    return lax.ppermute(x, axis, pairs)


def pool_weights_table():
    pixel_ids = jnp.arange(PIXELS, dtype=jnp.int32)
    row_of = pixel_ids // SIDE
    column = pixel_ids % SIDE
    pieces = []
    for extent in EXTENTS:
        across = SIDE // extent
        target = row_of // extent * across + column // extent
        member = jnp.arange(across * across, dtype=jnp.int32)[:, None] == target[None, :]
        pieces.append(member.astype(jnp.float32) / (extent * extent))
    return jnp.concatenate(pieces, 0)


def pool_back(cells):
    lead = cells.shape[0]
    chans = cells.shape[-1]
    total = None
    start = 0
    for extent in EXTENTS:
        across = SIDE // extent
        part = cells[:, start : start + across * across] * (1.0 / (extent * extent))
        start += across * across
        part = part.reshape(lead, across, 1, across, 1, chans)
        part = jnp.broadcast_to(part, (lead, across, extent, across, extent, chans))
        part = part.reshape(lead, PIXELS, chans)
        total = part if total is None else total + part
    return total


def local(features, neighbours, pairing, valid_tiles, cotangent):
    tile_count = features.shape[1]
    half_rows = cotangent.shape[2]
    pool_weights = pool_weights_table()
    present = lax.all_gather(features, "chan", axis=3, tiled=True)[0]
    before = shift(present, "frame", 1)
    after = shift(present, "frame", -1)
    partners = jnp.stack([before, after], 0)
    window = jnp.concatenate(
        [shift(partners, "tile", 1), partners, shift(partners, "tile", -1)], axis=1
    )
    pyramid = jnp.einsum(
        "mp,jwpc->jwmc",
        pool_weights.astype(jnp.bfloat16),
        window,
        preferred_element_type=jnp.float32,
    ).astype(jnp.bfloat16)
    gate01 = pairing[0].astype(jnp.bfloat16)
    pyramid = pyramid * gate01[:, None, None, None]
    core_index = lax.axis_index("chan")
    queries = lax.dynamic_slice_in_dim(present, core_index * half_rows, half_rows, 1)
    valid_local = lax.dynamic_slice_in_dim(valid_tiles, core_index * half_rows, half_rows, 1)
    scale = valid_local.astype(jnp.float32) * (1.0 / math.sqrt(CHANNELS))
    slot_ids = neighbours - (lax.axis_index("tile") * tile_count - tile_count)
    chosen = pyramid[:, slot_ids]
    queries2 = jnp.broadcast_to(queries[None], (2,) + queries.shape)
    per_tile = []
    for a in range(tile_count):
        tile_scores = jnp.einsum(
            "jkmc,jpc->kmp", chosen[:, a], queries2[:, a], preferred_element_type=jnp.float32
        )
        per_tile.append(tile_scores.reshape(NEIGHBOURS * LEVELS, half_rows) * scale[a][None])
    volume = jnp.stack(per_tile, 1).astype(jnp.bfloat16)
    volume = jnp.transpose(volume, (1, 2, 0))[None]
    upstream = cotangent[0].reshape(tile_count, half_rows, NEIGHBOURS, LEVELS)
    upstream = upstream * valid_local.astype(jnp.bfloat16)[:, :, None, None]
    partial_query = jnp.einsum(
        "apkm,jakmc->japc", upstream, chosen, preferred_element_type=jnp.float32
    )
    query_grad = jnp.sum(partial_query, axis=0) * (1.0 / math.sqrt(CHANNELS))
    base_grad = jnp.einsum("apkm,apc->akmc", upstream, queries, preferred_element_type=jnp.float32)
    member = (
        slot_ids[:, :, None] == jnp.arange(3 * tile_count, dtype=jnp.int32)[None, None, :]
    ).astype(jnp.float32)
    cells = None
    for a in range(tile_count):
        for k in range(NEIGHBOURS):
            term = member[a, k][:, None, None] * base_grad[a, k][None]
            cells = term if cells is None else cells + term
    window_grad = pool_back(cells)
    sent_left = shift(window_grad[:tile_count].astype(jnp.bfloat16), "tile", -1)
    sent_right = shift(window_grad[2 * tile_count :].astype(jnp.bfloat16), "tile", 1)
    returned = (
        sent_left.astype(jnp.float32)
        + window_grad[tile_count : 2 * tile_count]
        + sent_right.astype(jnp.float32)
    )
    gates = pairing[0].astype(jnp.float32) * (1.0 / math.sqrt(CHANNELS))
    from_next = shift((returned * gates[0]).astype(jnp.bfloat16), "frame", -1)
    from_prev = shift((returned * gates[1]).astype(jnp.bfloat16), "frame", 1)
    key_grad = from_prev.astype(jnp.float32) + from_next.astype(jnp.float32)
    placed = lax.dynamic_update_slice_in_dim(
        jnp.zeros(key_grad.shape, jnp.float32), query_grad, core_index * half_rows, 1
    )
    feature_grad = lax.psum_scatter(key_grad + placed, "chan", scatter_dimension=2, tiled=True)
    return (volume, feature_grad[None])


def solution(mesh):
    return jax.shard_map(
        local,
        mesh=mesh,
        in_specs=(
            P(("clip", "frame"), "tile", None, "chan"),
            P(("clip", "tile"), None),
            P(("clip", "frame"), None),
            P(("clip", "tile"), None),
            P(("clip", "frame"), "tile", "chan", None),
        ),
        out_specs=(
            P(("clip", "frame"), "tile", "chan", None),
            P(("clip", "frame"), "tile", None, "chan"),
        ),
        check_vma=False,
    )
```

```python
import math

import jax
import jax.numpy as jnp
from jax import lax
from jax.sharding import PartitionSpec as P

CHANNELS = 256
SIDE = 16
PIXELS = 256
LEVELS = 340
NEIGHBOURS = 9
EXTENTS = (1, 2, 4, 8)


def shift(x, axis, step):
    count = lax.axis_size(axis)
    if step > 0:
        pairs = [(i, i + 1) for i in range(count - 1)]
    else:
        pairs = [(i + 1, i) for i in range(count - 1)]
    return lax.ppermute(x, axis, pairs)


def pool_weights_table():
    pixel_ids = jnp.arange(PIXELS, dtype=jnp.int32)
    row_of = pixel_ids // SIDE
    column = pixel_ids % SIDE
    pieces = []
    for extent in EXTENTS:
        across = SIDE // extent
        target = row_of // extent * across + column // extent
        member = jnp.arange(across * across, dtype=jnp.int32)[:, None] == target[None, :]
        pieces.append(member.astype(jnp.float32) / (extent * extent))
    return jnp.concatenate(pieces, 0)


def pool_back(cells):
    lead = cells.shape[0]
    chans = cells.shape[-1]
    total = None
    start = 0
    for extent in EXTENTS:
        across = SIDE // extent
        part = cells[:, start : start + across * across] * (1.0 / (extent * extent))
        start += across * across
        part = part.reshape(lead, across, 1, across, 1, chans)
        part = jnp.broadcast_to(part, (lead, across, extent, across, extent, chans))
        part = part.reshape(lead, PIXELS, chans)
        total = part if total is None else total + part
    return total


def local(features, neighbours, pairing, valid_tiles, cotangent):
    tile_count = features.shape[1]
    half_rows = cotangent.shape[2]
    pool_weights = pool_weights_table()
    present = lax.all_gather(features, "chan", axis=3, tiled=True)[0]
    before = shift(present, "frame", 1)
    after = shift(present, "frame", -1)
    partners = jnp.stack([before, after], 0)
    window = jnp.concatenate(
        [shift(partners, "tile", 1), partners, shift(partners, "tile", -1)], axis=1
    )
    pyramid = jnp.einsum(
        "mp,jwpc->jwmc",
        pool_weights.astype(jnp.bfloat16),
        window,
        preferred_element_type=jnp.float32,
    ).astype(jnp.bfloat16)
    gate01 = pairing[0].astype(jnp.bfloat16)
    pyramid = pyramid * gate01[:, None, None, None]
    core_index = lax.axis_index("chan")
    queries = lax.dynamic_slice_in_dim(present, core_index * half_rows, half_rows, 1)
    valid_local = lax.dynamic_slice_in_dim(valid_tiles, core_index * half_rows, half_rows, 1)
    scale = valid_local.astype(jnp.float32) * (1.0 / math.sqrt(CHANNELS))
    slot_ids = neighbours - (lax.axis_index("tile") * tile_count - tile_count)
    chosen = pyramid[:, slot_ids]
    queries2 = jnp.broadcast_to(queries[None], (2,) + queries.shape)
    scores = jnp.einsum(
        "jakmc,japc->kmap", chosen, queries2, preferred_element_type=jnp.float32
    )
    summed = scores * scale[None, None]
    volume = summed.reshape(NEIGHBOURS * LEVELS, tile_count, half_rows).astype(jnp.bfloat16)
    volume = jnp.transpose(volume, (1, 2, 0))[None]
    upstream = cotangent[0] * valid_local.astype(jnp.bfloat16)[:, :, None]
    flat_chosen = chosen.reshape(2, tile_count, NEIGHBOURS * LEVELS, chosen.shape[-1])
    partial_query = jnp.einsum(
        "apn,janc->japc", upstream, flat_chosen, preferred_element_type=jnp.float32
    )
    query_grad = jnp.sum(partial_query, axis=0) * (1.0 / math.sqrt(CHANNELS))
    flat_grad = jnp.einsum("apn,apc->anc", upstream, queries, preferred_element_type=jnp.float32)
    base_grad = flat_grad.reshape(tile_count, NEIGHBOURS, LEVELS, flat_grad.shape[-1])
    member = (
        slot_ids[:, :, None] == jnp.arange(3 * tile_count, dtype=jnp.int32)[None, None, :]
    ).astype(jnp.float32)
    cells = None
    for a in range(tile_count):
        for k in range(NEIGHBOURS):
            term = member[a, k][:, None, None] * base_grad[a, k][None]
            cells = term if cells is None else cells + term
    window_grad = pool_back(cells)
    sent_left = shift(window_grad[:tile_count].astype(jnp.bfloat16), "tile", -1)
    sent_right = shift(window_grad[2 * tile_count :].astype(jnp.bfloat16), "tile", 1)
    returned = (
        sent_left.astype(jnp.float32)
        + window_grad[tile_count : 2 * tile_count]
        + sent_right.astype(jnp.float32)
    )
    gates = pairing[0].astype(jnp.float32) * (1.0 / math.sqrt(CHANNELS))
    from_next = shift((returned * gates[0]).astype(jnp.bfloat16), "frame", -1)
    from_prev = shift((returned * gates[1]).astype(jnp.bfloat16), "frame", 1)
    key_grad = from_prev.astype(jnp.float32) + from_next.astype(jnp.float32)
    placed = lax.dynamic_update_slice_in_dim(
        jnp.zeros(key_grad.shape, jnp.float32), query_grad, core_index * half_rows, 1
    )
    feature_grad = lax.psum_scatter(key_grad + placed, "chan", scatter_dimension=2, tiled=True)
    return (volume, feature_grad[None])


def solution(mesh):
    return jax.shard_map(
        local,
        mesh=mesh,
        in_specs=(
            P(("clip", "frame"), "tile", None, "chan"),
            P(("clip", "tile"), None),
            P(("clip", "frame"), None),
            P(("clip", "tile"), None),
            P(("clip", "frame"), "tile", "chan", None),
        ),
        out_specs=(
            P(("clip", "frame"), "tile", "chan", None),
            P(("clip", "frame"), "tile", None, "chan"),
        ),
        check_vma=False,
    )
```
